256 devices in a mesh: gx: 32 (over z, y_hi, core), gy: 8 (over x, y_lo).
Axes of the slice: x: 4, y: 4 (y_hi: 2, y_lo: 2; y = y_hi * 2 + y_lo), z: 8, core: 2. Of those that a mesh axis runs over, the one named last changes fastest.
Arguments:
- row_cells: int32 [8, 32, 4096], P('gy', 'gx'), may hold values from 0 to 255
- col_cells: int32 [8, 32, 4096], P('gy', 'gx'), may hold values from 0 to 255
- fracs: float32 [2, 8, 32, 4096], P(None, 'gy', 'gx'), may hold values from 0 to 1
- counts: int32 [8, 32], P('gy', 'gx'), may hold values from 512 to 4096, as said below
- targets: float32 [8, 32, 4096], P('gy', 'gx'), may hold values from -18 to 18
- amplitude: float32 [2048, 8192], P('gy', 'gx'), may hold values from 0.5 to 2
- lengthscale: float32 [2], replicated, may hold values from 51.2 to 64
- ridge: float32 [1], replicated, may hold values from 0.5 to 2
Outputs:
- solution: float32 [8, 32, 4096], P('gy', 'gx')
- residual: float32 [8, 32, 4096], P('gy', 'gx')
- relative: float32 [1], replicated
The draws below stay inside these ranges and needn't reach their ends.
Inputs may be any that keep to these rules, and one draw needn't show every extreme that they name: Slots 0 to counts - 1 of a tile are live; some tile holds 4096 live points.
All inputs are finite; a program needn't handle non-finite values.
Results may differ from the reference program's by a relative error of at most 0.0003.
Values sent between devices are 32-bit elements; how exact they have to be, the bound alone decides.
No kernel may reach another device: no remote copies, remote signals or barrier semaphores. Data moves between devices by JAX's collectives and lax.ppermute only.
A program may use at most 64 MiB of HBM per device.

```python
import math
import jax
import jax.numpy as jnp

CR = 256
CC = 256
P_SIZE = 4096
HB = 128
NR = 2048
NC = 8192
N_GX = 32
N_GY = 8


def draw_counts(key, part):
    total = N_GY * N_GX
    raw_draw = jax.random.randint(jax.random.fold_in(key, 11), (total,), 0, P_SIZE + 1)
    skewed = jnp.maximum(P_SIZE // 8, raw_draw * raw_draw // P_SIZE)
    chosen = jax.random.randint(jax.random.fold_in(key, 17), (), 0, total)
    tile_index = jnp.arange(total, dtype=jnp.int32)
    return jnp.where(tile_index == chosen, P_SIZE, skewed).astype(jnp.int32).reshape(N_GY, N_GX)


def draw_targets(key, part):
    tiles = N_GY * N_GX
    order = (jnp.arange(N_GY)[:, None] * N_GX + jnp.arange(N_GX)[None, :]).astype(jnp.float32)
    rising = 1.0 + 2.0 * order / max(tiles - 1, 1)
    noise = jax.random.truncated_normal(jax.random.fold_in(key, 29), -6.0, 6.0, (N_GY, N_GX, P_SIZE), jnp.float32)
    return noise * rising[:, :, None]


def set_ends(array, rng, least, high):
    longest = array.shape.index(max(array.shape))
    spots = []
    for shift in (0, 1):
        where = [jax.random.randint(jax.random.fold_in(rng, axis), (), 0, length) for axis, length in enumerate(array.shape)]
        where[longest] = (where[longest] + shift) % array.shape[longest]
        spots.append(tuple(where))
    return array.at[spots[0]].set(least).at[spots[1]].set(high)


def block_scale(stream_key, dims, shards, smallest, top_value):
    def one(axis_at, shards_of):
        heights = jax.random.uniform(jax.random.fold_in(jax.random.fold_in(stream_key, 6), axis_at), (shards_of,), jnp.float32, smallest / len(shards), top_value / len(shards))
        return jnp.repeat(jnp.exp(heights), dims[axis_at] // shards_of).reshape((-1,) + (1,) * (len(dims) - axis_at - 1))

    level = one(*shards[0])
    for cut in shards[1:]:
        level = level * one(*cut)
    return level


def setup_inputs(seed: int = 0) -> dict:
    seeds = jax.random.split(jax.random.key(seed), 9)
    row_cells = set_ends(jax.random.randint(seeds[0], (N_GY, N_GX, P_SIZE), 0, CR), jax.random.fold_in(seeds[0], 1), 0, CR - 1).astype(jnp.int32)
    col_cells = set_ends(jax.random.randint(seeds[1], (N_GY, N_GX, P_SIZE), 0, CC), jax.random.fold_in(seeds[1], 1), 0, CC - 1).astype(jnp.int32)
    fracs = jnp.clip(1.0 * jax.random.uniform(seeds[2], (2, N_GY, N_GX, P_SIZE), jnp.float32) ** block_scale(seeds[2], (2, N_GY, N_GX, P_SIZE), ((1, 8), (2, 32)), -0.2, 0.2), 0.0, 1.0)
    counts = draw_counts(jax.random.fold_in(seeds[8], 71), 0)
    targets = draw_targets(jax.random.fold_in(seeds[8], 71), 0)
    amplitude = jnp.clip(jnp.exp(math.log(2.0) - 1.3862944 * jax.random.uniform(seeds[5], (NR, NC), jnp.float32) ** block_scale(seeds[5], (NR, NC), ((0, 8), (1, 32)), -0.2, 0.2)), 0.5, 2.0)
    lengthscale = jnp.clip(jnp.exp(jax.random.uniform(seeds[6], (2,), jnp.float32, math.log(51.2), math.log(64.0))), 51.2, 64.0)
    ridge = jnp.clip(jnp.exp(jax.random.uniform(seeds[7], (1,), jnp.float32, math.log(0.5), math.log(2.0))), 0.5, 2.0)
    return {"row_cells": row_cells, "col_cells": col_cells, "fracs": fracs, "counts": counts, "targets": targets, "amplitude": amplitude, "lengthscale": lengthscale, "ridge": ridge}


def cubic_weights(fraction):
    square = fraction * fraction
    cube = square * fraction
    return (-0.5 * cube + square - 0.5 * fraction,
            1.5 * cube - 2.5 * square + 1.0,
            -1.5 * cube + 2.0 * square + 0.5 * fraction,
            0.5 * cube - 0.5 * square)


def periodic_conv(field, scale, axis):
    length = field.shape[axis]
    offset_idx = jnp.arange(length, dtype=jnp.int32)
    distance = jnp.minimum(offset_idx, length - offset_idx).astype(field.dtype)
    taps = jnp.where(distance <= HB, jnp.exp(-distance * distance / (2.0 * scale * scale)), 0.0)
    spectrum = jnp.fft.rfft(field, axis=axis) * jnp.expand_dims(jnp.fft.rfft(taps), 1 - axis)
    return jnp.fft.irfft(spectrum, n=length, axis=axis).astype(field.dtype)


def reference(row_cells, col_cells, fracs, counts, targets, amplitude, lengthscale, ridge):
    tile_rows = jnp.arange(N_GY, dtype=jnp.int32)[:, None, None]
    tile_cols = jnp.arange(N_GX, dtype=jnp.int32)[None, :, None]
    slot_index = jnp.arange(P_SIZE, dtype=jnp.int32)[None, None, :]
    live_slots = (slot_index < counts[:, :, None]).astype(jnp.float32)
    row_weights = cubic_weights(fracs[0])
    col_weights = cubic_weights(fracs[1])
    row_index = [((tile_rows * CR + row_cells + offset - 1) % NR).astype(jnp.int32) for offset in range(4)]
    col_index = [((tile_cols * CC + col_cells + offset - 1) % NC).astype(jnp.int32) for offset in range(4)]

    def spread(vector):
        flat = jnp.zeros((NR * NC,), jnp.float32)
        for row_step in range(4):
            for col_step in range(4):
                where_to = (row_index[row_step] * NC + col_index[col_step]).reshape(-1)
                amount = vector * live_slots * row_weights[row_step] * col_weights[col_step]
                flat = flat.at[where_to].add(amount.reshape(-1))
        return flat.reshape(NR, NC)

    def gather_back(grid_values):
        total = jnp.zeros(vector_shape, jnp.float32)
        for row_step in range(4):
            for col_step in range(4):
                total = total + row_weights[row_step] * col_weights[col_step] * grid_values[row_index[row_step], col_index[col_step]]
        return total * live_slots

    vector_shape = targets.shape

    def operate(vector):
        field = amplitude * spread(vector)
        smooth = periodic_conv(periodic_conv(field, lengthscale[1], 1), lengthscale[0], 0)
        return gather_back(amplitude * smooth) + ridge[0] * vector

    right_side = targets * live_slots
    norm_start = jnp.sum(right_side * right_side)
    image = operate(right_side)
    step_one = norm_start / jnp.sum(right_side * image)
    solution_one = step_one * right_side
    residual_one = right_side - step_one * image
    norm_mid = jnp.sum(residual_one * residual_one)
    direction = residual_one + (norm_mid / norm_start) * right_side
    image_two = operate(direction)
    step_two = norm_mid / jnp.sum(direction * image_two)
    solution = solution_one + step_two * direction
    residual = residual_one - step_two * image_two
    relative = (jnp.sum(residual * residual) / norm_start).reshape(1)
    return solution, residual, relative
```

```python
import jax
import jax.numpy as jnp
from jax import lax
from jax.experimental import pallas as pl
from jax.experimental.pallas import tpu as pltpu
from jax.sharding import PartitionSpec as P

f32 = jnp.float32
bf16 = jnp.bfloat16
HB = 128
T = 256
E = 264
L = 384
H = 144
K = E + 2 * H
STEP = 512
MM = (((1,), (0,)), ((), ()))
MT = (((1,), (1,)), ((), ()))


def dot(left, right, dims):
    return lax.dot_general(left, right, dims, preferred_element_type=f32)


def split(x):
    high = x.astype(bf16)
    return high, (x - high.astype(f32)).astype(bf16)


def cell_of(slot):
    return jnp.where(slot <= T + 1, slot, jnp.where(slot == T + 2, -1, -100000))


def cubic_weights(fraction):
    square = fraction * fraction
    cube = square * fraction
    return (
        -0.5 * cube + square - 0.5 * fraction,
        1.5 * cube - 2.5 * square + 1.0,
        -1.5 * cube + 2.0 * square + 0.5 * fraction,
        0.5 * cube - 0.5 * square,
    )


def stencil(cells, fraction, live=None):
    w = cubic_weights(fraction)
    if live is not None:
        w = tuple(x * live for x in w)
    d = cell_of(lax.broadcasted_iota(jnp.int32, (E, cells.shape[1]), 0)) - (cells - 1)
    return jnp.where(
        d == 0, w[0], jnp.where(d == 1, w[1], jnp.where(d == 2, w[2], jnp.where(d == 3, w[3], 0.0)))
    )


def stencils(i, rows, cols, fracs, count):
    at = pl.ds(i * STEP, STEP)
    slot = lax.broadcasted_iota(jnp.int32, (1, STEP), 1) + i * STEP
    live = (slot < count[0, 0]).astype(f32)
    return (
        at,
        live,
        stencil(rows[:, at], fracs[0:1, at], live),
        stencil(cols[:, at], fracs[1:2, at]),
    )


def add_spread(i, weighted, r, out, edge):
    ch, cl = split(weighted)
    rh, rl = split(r[:T])
    main = dot(ch, rh, MT) + dot(ch, rl, MT) + dot(cl, rh, MT)
    tail = r[T:]
    tail_high = tail.astype(bf16).astype(f32)
    pair = jnp.concatenate([tail_high, tail - tail_high], 0).astype(bf16)
    first = dot(ch, pair, MT)
    side = first[:, :8] + first[:, 8:] + dot(cl, pair, MT)[:, :8]
    if i == 0:
        edge[...] = jnp.zeros_like(edge)
        out[:, :T] = main
        edge[:, :8] = side
    else:
        out[:, :T] += main
        edge[:, :8] += side


def pick_parts(g):
    gh, gl = split(g[:, :T])
    tail = g[:, T : T + 8]
    tail_high = tail.astype(bf16).astype(f32)
    tail_low = tail - tail_high
    pack = jnp.concatenate([tail_high, tail_high, tail_low, jnp.zeros_like(tail)], 1).astype(bf16)
    return gh, gl, pack


def pick(parts, c, r):
    gh, gl, pack = parts
    ch, cl = split(c[:T])
    tail = c[T:]
    tail_high = tail.astype(bf16).astype(f32)
    tall = jnp.concatenate([tail_high, tail - tail_high, tail_high, jnp.zeros_like(tail)], 0)
    value = dot(gh, ch, MM) + dot(gh, cl, MM) + dot(gl, ch, MM) + dot(pack, tall.astype(bf16), MM)
    return jnp.sum(value * r, axis=0, keepdims=True)


def write_slabs(x, even, far, near):
    low = jnp.concatenate([x[: H - 8], x[T:E]], 0)
    high = x[E - H : E]
    far[:H] = jnp.where(even, low, high)
    near[:H] = jnp.where(even, high, low)


def edge_rows(x):
    row = lax.broadcasted_iota(jnp.int32, (8, x.shape[1]), 0)
    return jnp.where(row < 2, x[0:8], jnp.broadcast_to(x[T - 1 : T], (8, x.shape[1])))


def outside_rows(even, far, near):
    row = lax.broadcasted_iota(jnp.int32, far.shape, 0)
    before = jnp.where(even, far, near)
    after = jnp.where(even, near, far)
    return jnp.where(row < 2, after, jnp.where(row == 2, before, 0.0))


def smooth_by(bands, x):
    high, low = split(x)
    return dot(bands[0], high, MM) + dot(bands[0], low, MM) + dot(bands[1], high, MM)


def band(even, scale, high, low):
    out = cell_of(lax.broadcasted_iota(jnp.int32, (E, K), 0))
    k = lax.broadcasted_iota(jnp.int32, (E, K), 1)
    is_far = jnp.logical_and(k >= E, k < E + H)
    from_before = is_far == even
    j = jnp.where(k < E, k, jnp.where(is_far, k - E, k - E - H))
    slab = jnp.where(jnp.logical_or(from_before, j >= H - 8), j + (E - H), j)
    cell = cell_of(jnp.where(k < E, k, slab))
    source = jnp.where(k < E, cell, jnp.where(from_before, cell - T, cell + T))
    d = jnp.abs(source - out)
    distance = d.astype(f32)
    value = jnp.where(
        jnp.logical_and(d <= HB, out >= -1),
        jnp.exp(-distance * distance / (2.0 * scale * scale)),
        0.0,
    )
    high[...], low[...] = split(value)


def bands_kernel(place, scales, xh, xl, yh, yl):
    band(place[0] == 0, scales[1], xh, xl)
    band(place[1] == 0, scales[0], yh, yl)


def spread_kernel(rows, cols, fracs, count, targets, out, right, edge):
    for i in range(rows.shape[1] // STEP):
        at, live, r, c = stencils(i, rows, cols, fracs, count)
        vector = targets[:, at] * live
        right[:, at] = vector
        add_spread(i, c * vector, r, out, edge)
    out[:, T:] = edge[...]


def first_slabs_kernel(place, spread, amplitude, far_edge, near_edge, scaled, across_scale, far, near):
    ends = outside_rows(place[1] == 0, far_edge[...], near_edge[...])
    wide = jnp.concatenate([amplitude[...], ends, jnp.zeros((L - E, T), f32)], 0)
    scale = jnp.transpose(wide)
    across_scale[...] = scale
    scaled[:T] = spread[:T] * scale
    scaled[T:] = spread[T:]
    write_slabs(scaled[...], place[0] == 0, far, near)
    edges = edge_rows(scale)
    far[H:] = edges
    near[H:] = edges


def across_body(place, scaled, scale, ends, far, near, bands, across, far_out, near_out):
    edges = edge_rows(scale)
    field = jnp.concatenate(
        [
            scaled[:T],
            scaled[T:] * ends,
            far[: H - 8],
            far[H - 8 : H] * edges,
            near[: H - 8],
            near[H - 8 : H] * edges,
        ],
        0,
    )
    smoothed = smooth_by(bands, field)
    turned = jnp.transpose(jnp.concatenate([smoothed, jnp.zeros((L - E, L), f32)], 0))[:E]
    across[...] = turned
    write_slabs(turned, place[1] == 0, far_out, near_out)


def first_across_kernel(place, scaled, scale, far, near, xh, xl, across, far_out, near_out, ends, grid_scale):
    outside = outside_rows(place[0] == 0, far[H:], near[H:])
    ends[...] = outside
    whole = jnp.concatenate([scale[...], outside, jnp.zeros((L - E, L), f32)], 0)
    grid_scale[...] = jnp.transpose(whole)[:E]
    across_body(
        place, scaled[...], scale[...], outside, far[...], near[...], (xh[...], xl[...]), across, far_out, near_out
    )


def across_kernel(place, scaled, scale, ends, far, near, xh, xl, across, far_out, near_out):
    across_body(
        place, scaled[...], scale[...], ends[...], far[...], near[...], (xh[...], xl[...]), across, far_out, near_out
    )


def grid_parts(across, far, near, yh, yl, grid_scale):
    field = jnp.concatenate([across[...], far[...], near[...]], 0)
    return pick_parts(smooth_by((yh[...], yl[...]), field) * grid_scale[...])


def middle_kernel(
    place, count, across, far, near, yh, yl, grid_scale, rows, cols, fracs, scale,
    image, scaled, far_out, near_out, edge,
):
    parts = grid_parts(across, far, near, yh, yl, grid_scale)
    for i in range(rows.shape[1] // STEP):
        at, _, r, c = stencils(i, rows, cols, fracs, count)
        value = pick(parts, c, r)
        image[:, at] = value
        add_spread(i, c * value, r, scaled, edge)
    scaled[:, T:] = edge[...]
    scaled[:T] = scaled[:T] * scale[...]
    write_slabs(scaled[...], place[0] == 0, far_out, near_out)


def last_kernel(
    count, across, far, near, yh, yl, grid_scale, rows, cols, fracs, right, image,
    image_two, sums,
):
    parts = grid_parts(across, far, near, yh, yl, grid_scale)
    for i in range(rows.shape[1] // STEP):
        at, _, r, c = stencils(i, rows, cols, fracs, count)
        image_two[:, at] = pick(parts, c, r)
    b, v, w = right[...], image[...], image_two[...]
    lane = lax.broadcasted_iota(jnp.int32, (1, 128), 1)
    total = jnp.zeros((1, 128), f32)
    for i, product in enumerate((b * b, b * v, v * v, v * w, w * w)):
        total = jnp.where(lane == i, jnp.sum(product, axis=1, keepdims=True), total)
    sums[...] = total


def finish_kernel(ridge, parts, right, image, image_two, solution_out, residual_out, relative_out):
    total = jnp.sum(parts[...], axis=0, keepdims=True)
    bb, bv, vv, vw, ww = (total[:, i : i + 1] for i in range(5))
    rho = ridge[0]
    b_image = bv + rho * bb
    one = bb / b_image
    keep = 1.0 - one * rho
    mid = keep * keep * bb - 2.0 * keep * one * bv + one * one * vv
    curve = keep * keep * bv - 2.0 * keep * one * vv + one * one * vw
    ratio = mid / bb
    two = mid / (curve + rho * mid - ratio * mid / one)
    side = keep + ratio
    on_b = keep - two * rho * side
    on_v = -one - two * (side - rho * one)
    on_w = two * one
    b, v, w = right[...], image[...], image_two[...]
    solution_out[...] = (one + two * side) * b - (two * one) * v
    residual_out[...] = on_b * b + on_v * v + on_w * w
    end = (
        on_b * on_b * bb
        + 2.0 * on_b * on_v * bv
        + (on_v * on_v + 2.0 * on_b * on_w) * vv
        + 2.0 * on_v * on_w * vw
        + on_w * on_w * ww
    )
    relative_out[...] = jnp.broadcast_to(end / bb, relative_out.shape)


def call(kernel, outs, args, scalars, scratch=(), mib=20, flops=0):
    vmem = pl.BlockSpec(memory_space=pltpu.VMEM)
    smem = pl.BlockSpec(memory_space=pltpu.SMEM)
    shapes = tuple(jax.ShapeDtypeStruct(shape, dtype) for shape, dtype in outs)
    return pl.pallas_call(
        kernel,
        out_shape=shapes,
        in_specs=[smem if i in scalars else vmem for i in range(len(args))],
        out_specs=tuple(vmem for _ in outs),
        scratch_shapes=list(scratch),
        compiler_params=pltpu.CompilerParams(vmem_limit_bytes=mib << 20),
        cost_estimate=pl.CostEstimate(flops=flops, bytes_accessed=1 << 20, transcendentals=0),
    )(*args)


def solution(mesh):
    gx, gy = mesh.axis_names

    def pairs(axis):
        count = mesh.shape[axis]
        near = [(i, i ^ 1) for i in range(count)]
        far = [(i, (i + 1) % count if i % 2 else (i - 1) % count) for i in range(count)]
        return far, near

    def swap(axis, far, near):
        far_to, near_to = pairs(axis)
        return lax.ppermute(far, axis, far_to), lax.ppermute(near, axis, near_to)

    def shards(row_cells, col_cells, fracs, counts, targets, amplitude, lengthscale, ridge):
        n = targets.shape[2]
        rows, cols = row_cells.reshape(1, n), col_cells.reshape(1, n)
        fracs = fracs.reshape(2, n)
        place = jnp.stack([lax.axis_index(gx) % 2, lax.axis_index(gy) % 2]).astype(jnp.int32)
        edge = pltpu.VMEM((E, L - T), f32)
        vector = ((1, n), f32)
        grid = ((E, L), f32)
        slab = ((H, L), f32)
        tall = ((H + 8, L), f32)
        band_part = ((E, K), bf16)

        ends = jnp.concatenate([amplitude[0:2], amplitude[T - 1 : T], jnp.zeros((5, T), f32)], 0)
        far_end, near_end = swap(gy, ends, ends)
        xh, xl, yh, yl = call(bands_kernel, (band_part,) * 4, (place, lengthscale), (0, 1))
        spread, right = call(
            spread_kernel,
            (grid, vector),
            (rows, cols, fracs, counts, targets.reshape(1, n)),
            (3,),
            (edge,),
            flops=6 << 28,
        )
        scaled, scale, far, near = call(
            first_slabs_kernel,
            (grid, ((T, L), f32), tall, tall),
            (place, spread, amplitude, far_end, near_end),
            (0,),
        )
        far, near = swap(gx, far, near)
        across, far, near, outside, grid_scale = call(
            first_across_kernel,
            (grid, slab, slab, ((8, L), f32), grid),
            (place, scaled, scale, far, near, xh, xl),
            (0,),
        )
        far, near = swap(gy, far, near)
        image, scaled, far, near = call(
            middle_kernel,
            (vector, grid, slab, slab),
            (place, counts, across, far, near, yh, yl, grid_scale, rows, cols, fracs, scale),
            (0, 1),
            (edge,),
        )
        far, near = swap(gx, far, near)
        across, far, near = call(
            across_kernel,
            (grid, slab, slab),
            (place, scaled, scale, outside, far, near, xh, xl),
            (0,),
        )
        far, near = swap(gy, far, near)
        image_two, sums = call(
            last_kernel,
            (vector, ((1, 128), f32)),
            (counts, across, far, near, yh, yl, grid_scale, rows, cols, fracs, right, image),
            (0,),
        )
        devices = mesh.size
        copies = jnp.broadcast_to(sums[None], (devices, 1, 128))
        parts = lax.all_to_all(copies, (gx, gy), 0, 0).reshape(devices, 128)
        out, residual, relative = call(
            finish_kernel,
            (vector, vector, ((1, 128), f32)),
            (ridge, parts, right, image, image_two),
            (0,),
        )
        return out.reshape(1, 1, n), residual.reshape(1, 1, n), relative[0, :1]

    tiles = P(gy, gx, None)
    return jax.shard_map(
        shards,
        mesh=mesh,
        in_specs=(tiles, tiles, P(None, gy, gx, None), P(gy, gx), tiles, P(gy, gx), P(), P()),
        out_specs=(tiles, tiles, P()),
        check_vma=False,
    )
```

```python
import jax
import jax.numpy as jnp
from jax import lax
from jax.experimental import pallas as pl
from jax.experimental.pallas import tpu as pltpu
from jax.sharding import PartitionSpec as P

f32 = jnp.float32
bf16 = jnp.bfloat16
HB = 128
T = 256
HALF = T // 2
E = T + 8
TALL = T + 16
SLAB = HALF + 16
FIELD = 2 * T + 24
K = 2 * T + 128
STEP = 512
MM = (((1,), (0,)), ((), ()))
MT = (((1,), (1,)), ((), ()))


def dot(left, right, dims):
    return lax.dot_general(left, right, dims, preferred_element_type=f32)


def split(x):
    high = x.astype(bf16)
    return high, (x - high.astype(f32)).astype(bf16)


def split_rows(x):
    high = x.astype(bf16).astype(f32)
    return jnp.concatenate([high, x - high], 0).astype(bf16)


def iota(shape, dim):
    return lax.broadcasted_iota(jnp.int32, shape, dim)


def cell_of(slot):
    return jnp.where(slot <= T + 1, slot, jnp.where(slot == T + 2, -1, -9999))


def cubic_weights(fraction):
    square = fraction * fraction
    cube = square * fraction
    return (
        -0.5 * cube + square - 0.5 * fraction,
        1.5 * cube - 2.5 * square + 1.0,
        -1.5 * cube + 2.0 * square + 0.5 * fraction,
        0.5 * cube - 0.5 * square,
    )


def slots(first, count, wrap):
    cell = cell_of(first + iota((count, 128), 0) % wrap).astype(jnp.int16)
    return jnp.concatenate([cell] * (STEP // 128), 1)


def place(cell, targets, weights):
    hits = [cell == target for target in targets]
    out = []
    for group in weights:
        value = jnp.zeros(cell.shape, bf16)
        for hit, weight in zip(hits, group):
            value = jnp.where(hit, jnp.broadcast_to(weight, cell.shape), value)
        out.append(value)
    return out


def touched(cells):
    return [(cells + (j - 1)).astype(jnp.int16) for j in range(4)]


def weight_parts(fraction, factor=None):
    pairs = [split(w if factor is None else w * factor) for w in cubic_weights(fraction)]
    return [high for high, _ in pairs], [low for _, low in pairs]


class Rows:
    def __init__(self):
        self.main = slots(0, T, T)
        self.tail = slots(T, 16, 16)
        self.twice = slots(T, 16, 8)
        self.upper = iota((16, STEP), 0) < 8

    def pair(self, targets, weights):
        high, low = place(self.twice, targets, weights)
        return jnp.where(self.upper, high.astype(f32), low.astype(f32)).astype(bf16)


def add_spread(i, rows, r_main, r_pair, targets, weights, out, edge):
    main, tail = place(rows.main, targets, weights), place(rows.tail, targets, weights)
    high, low = (jnp.concatenate([x, y], 0) for x, y in zip(main, tail))
    inner = dot(high, r_main[0], MT) + dot(high, r_main[1], MT) + dot(low, r_main[0], MT)
    first = dot(r_pair, high, MT)
    side = first[:8] + first[8:] + dot(r_pair, low, MT)[:8]
    if i == 0:
        edge[...] = jnp.zeros_like(edge)
        out[...] = inner[:E]
        edge[:, :TALL] = side
    else:
        out[...] += inner[:E]
        edge[:, :TALL] += side


def pick(grid, c_main, c_pair, r):
    high, low, tail = grid
    pack = jnp.concatenate([c_pair, c_pair], 0)
    value = dot(high, c_main[0], MM) + dot(high, c_main[1], MM) + dot(low, c_main[0], MM)
    value = value + dot(tail, pack, MM)
    return jnp.sum(value * r, axis=0, keepdims=True)


def put(row, value, index, x):
    return jnp.where(row == index, jnp.broadcast_to(value, x.shape), x)


def group_low(x, tail, dim):
    row = iota(tail.shape, dim)
    at = (lambda i: x[i : i + 1]) if dim == 0 else (lambda i: x[:, i : i + 1])
    return put(row, at(HALF), 6, put(row, at(HALF + 1), 7, tail))


def group_high(x, tail, dim):
    row = iota(tail.shape, dim)
    at = (lambda i: x[i : i + 1]) if dim == 0 else (lambda i: x[:, i : i + 1])
    return put(row, at(HALF - 1), 7, tail)


def edge_rows(x):
    row = iota((8, x.shape[1]), 0)
    return jnp.where(row < 2, x[:8], jnp.broadcast_to(x[T - 1 : T], row.shape))


def outside_rows(even, far, near):
    row = iota(far.shape, 0)
    before = jnp.where(even, far, near)
    after = jnp.where(even, near, far)
    return jnp.where(row < 2, after, jnp.where(row == 2, before, 0.0))


def outside_lanes(even, far, near):
    lane = iota((8, 128), 1)
    before = jnp.where(even, far, near)
    after = jnp.where(even, near, far)
    last = jnp.broadcast_to(before[:, T - 1 : T], lane.shape)
    return jnp.where(lane < 2, after[:, :128], jnp.where(lane == 2, last, 0.0))


def column_slabs(even, main, edge, far, near):
    tail = main[T:]
    low_rows, high_rows = group_low(main, tail, 0), group_high(main, tail, 0)
    lanes = edge[:, T:]
    low_lanes, high_lanes = group_low(edge, lanes, 1), group_high(edge, lanes, 1)
    for ref, low, shift in ((far, even, 8), (near, jnp.logical_not(even), 16)):
        ref[:HALF] = jnp.where(low, main[:HALF], main[HALF:T])
        ref[HALF : HALF + 8] = jnp.where(low, low_rows, high_rows)
        ref[HALF + 8 : SLAB, :128] = jnp.where(low, edge[:, :HALF], edge[:, HALF:T])
        group = jnp.where(low, low_lanes, high_lanes)
        group = jnp.where(iota(group.shape, 1) < 8, group, 0.0)
        ref[HALF + 8 : SLAB, 128:] = pltpu.roll(group, shift, 1)


def row_slabs(even, main, group, tail, far, near):
    low_rows, high_rows = group_low(main, group, 0), group_high(main, group, 0)
    for ref, low in ((far, even), (near, jnp.logical_not(even))):
        ref[:HALF] = jnp.where(low, main[:HALF, :T], main[HALF:, :T])
        rows = jnp.where(low, low_rows, high_rows)
        ref[HALF : HALF + 8] = rows[:, :T]
        ref[HALF + 8 : SLAB, :128] = jnp.where(low, tail[:, :HALF], tail[:, HALF:])
        ref[HALF + 8 : SLAB, 128:] = rows[:, T:]


def smooth_by(bands, x):
    high, low = split(x)
    return dot(bands[0], high, MM) + dot(bands[0], low, MM) + dot(bands[1], high, MM)


def band(even, scale, high, low):
    out = cell_of(iota((E, K), 0))
    k = iota((E, K), 1)
    j = k - 2 * T
    is_own = jnp.logical_or(k < T, jnp.logical_and(j >= 0, j < 8))
    is_far = jnp.logical_or(
        jnp.logical_and(k >= T, k < T + HALF), jnp.logical_and(j >= 8, j < 16)
    )
    before = is_far == even
    g = j % 8
    extra = jnp.where(before, jnp.where(g == 7, HALF - 1, -9999), g + (HALF - 6))
    extra = jnp.where(jnp.logical_or(is_own, g < 6), -9999, extra)
    group = jnp.where(g < 3, cell_of(T + g), extra)
    inner = jnp.where(is_own, k, k % HALF + jnp.where(before, HALF, 0))
    cell = jnp.where(j < 0, inner, jnp.where(j < 24, group, -9999))
    source = jnp.where(is_own, cell, jnp.where(before, cell - T, cell + T))
    d = jnp.abs(source - out)
    distance = d.astype(f32)
    value = jnp.where(
        jnp.logical_and(d <= HB, out >= -1),
        jnp.exp(-distance * distance / (2.0 * scale * scale)),
        0.0,
    )
    high[...], low[...] = split(value)


def bands_kernel(spot, scales, xh, xl, yh, yl):
    band(spot[0] == 0, scales[1], xh, xl)
    band(spot[1] == 0, scales[0], yh, yl)


def fields(points, at):
    cells = [points[i : i + 1, at].astype(jnp.int32) for i in range(2)]
    return cells + [points[i : i + 1, at] for i in range(2, 6)]


def spread_kernel(points, out, edge):
    kinds = Rows()
    for i in range(points.shape[1] // STEP):
        at = pl.ds(i * STEP, STEP)
        rows, cols, row_fracs, col_fracs, live, vector = fields(points, at)
        r_at, r_weights = touched(rows), weight_parts(row_fracs, live)
        r_main = place(kinds.main, r_at, r_weights)
        r_pair = kinds.pair(r_at, r_weights)
        c_weights = weight_parts(col_fracs, vector)
        add_spread(i, kinds, r_main, r_pair, touched(cols), c_weights, out, edge)


def scaled_slabs(even, main, edge, turned, ends, main_out, edge_out, far, near):
    main_out[:T] = main[:T] * turned[...]
    main_out[T:] = main[T:]
    edge_out[:, :T] = edge[:, :T] * ends
    edge_out[:, T:] = edge[:, T:]
    column_slabs(even, main_out[...], edge_out[...], far, near)


def first_slabs_kernel(
    spot, main, edge, amplitude, far_ends, near_ends, main_out, edge_out, turned, ends, far, near
):
    row = iota((8, T), 0)
    far_rows, near_rows = (
        jnp.where(row < 2, x[:8], jnp.broadcast_to(x[15:], row.shape)) for x in (far_ends, near_ends)
    )
    ends[...] = outside_rows(spot[1] == 0, far_rows, near_rows)
    turned[...] = jnp.transpose(amplitude[...])
    scaled_slabs(
        spot[0] == 0, main[...], edge[...], turned, ends[...], main_out, edge_out, far, near
    )
    for ref in (far, near):
        ref[SLAB : SLAB + 8] = edge_rows(turned[...])
        ref[SLAB + 8 :] = ends[...]


def across_body(even_row, main, edge, turned, ends, outside, corner, far, near, bands, outs):
    row_out, group_out, tail_out, far_out, near_out = outs
    row = iota((8, T), 0)
    edges = jnp.where(row < 3, edge_rows(turned), 1.0)
    field = jnp.concatenate(
        [
            main[:T],
            far[:HALF],
            near[:HALF],
            main[T:] * outside,
            far[HALF : HALF + 8] * edges,
            near[HALF : HALF + 8] * edges,
        ],
        0,
    )
    smoothed = smooth_by((bands[0][:, :FIELD], bands[1][:, :FIELD]), field)
    lane = iota((8, 128), 1)
    g = lane % 8
    first, second = (jnp.broadcast_to(ends[:, i : i + 1], lane.shape) for i in (0, 1))
    third = jnp.broadcast_to(ends[:, T - 1 : T], lane.shape)
    factor = jnp.where(g == 0, first, jnp.where(g == 1, second, jnp.where(g == 2, third, 1.0)))
    factor = jnp.where(lane < 8, corner, factor)
    own = jnp.where(lane < 8, edge[:, T:], 0.0)
    groups = (own + far[HALF + 8 : SLAB, 128:] + near[HALF + 8 : SLAB, 128:]) * factor
    strip = jnp.concatenate(
        [edge[:, :T], far[HALF + 8 : SLAB, :128], near[HALF + 8 : SLAB, :128], groups], 1
    )
    pair = split_rows(strip)
    by_high = dot(pair, bands[0], MT)
    group = by_high[:8] + by_high[8:] + dot(pair, bands[1], MT)[:8]
    group = jnp.concatenate([group, jnp.zeros((8, 384 - E), f32)], 1)
    turned_back = jnp.transpose(jnp.concatenate([smoothed, jnp.zeros((384 - E, T), f32)], 0))
    row_out[...] = turned_back
    group_out[...] = group
    tail_out[...] = smoothed[T:]
    row_slabs(even_row, turned_back, group, smoothed[T:], far_out, near_out)


def first_across_kernel(
    spot, main, edge, amplitude, turned, ends, far, near, xh, xl,
    row_out, group_out, tail_out, far_out, near_out, outside, corner, scale, scale_tail,
):
    even = spot[0] == 0
    outside[...] = outside_rows(even, far[SLAB : SLAB + 8], near[SLAB : SLAB + 8])
    corner[...] = outside_lanes(even, far[SLAB + 8 :], near[SLAB + 8 :])
    scale[:T] = amplitude[...]
    scale[T:] = ends[...]
    wide = jnp.concatenate([outside[...], jnp.zeros((120, T), f32)], 0)
    scale_tail[:T] = jnp.transpose(wide)
    scale_tail[T:] = corner[...]
    across_body(
        spot[1] == 0, main[...], edge[...], turned[...], ends[...], outside[...], corner[...],
        far[...], near[...], (xh[...], xl[...]), (row_out, group_out, tail_out, far_out, near_out),
    )


def across_kernel(
    spot, main, edge, turned, ends, outside, corner, far, near, xh, xl,
    row_out, group_out, tail_out, far_out, near_out,
):
    across_body(
        spot[1] == 0, main[...], edge[...], turned[...], ends[...], outside[...], corner[...],
        far[...], near[...], (xh[...], xl[...]), (row_out, group_out, tail_out, far_out, near_out),
    )


def grid_parts(row, group, tail, far, near, yh, yl, scale, scale_tail):
    far_group, near_group = far[HALF : HALF + 8], near[HALF : HALF + 8]
    field = jnp.concatenate(
        [row[:, :T], far[:HALF], near[:HALF], group[:, :T], far_group, near_group], 0
    )
    main = smooth_by((yh[:, :FIELD], yl[:, :FIELD]), field) * scale[...]
    strip = jnp.concatenate(
        [tail[...], far[HALF + 8 : SLAB, :128], near[HALF + 8 : SLAB, :128]], 1
    )
    pair = split_rows(strip)
    by_high = dot(yh[:, : 2 * T], pair, MT)
    side = by_high[:, :8] + by_high[:, 8:] + dot(yl[:, : 2 * T], pair, MT)[:, :8]
    ends = jnp.concatenate(
        [group[:, T:], far[HALF + 8 : SLAB, 128:], near[HALF + 8 : SLAB, 128:]], 0
    )
    side = side + smooth_by((yh[:, 2 * T : FIELD], yl[:, 2 * T : FIELD]), ends)[:, :8]
    side = side * scale_tail[:, :8]
    high, low = split(main)
    side_high = side.astype(bf16).astype(f32)
    side_low = side - side_high
    zero = jnp.zeros_like(side)
    return high, low, jnp.concatenate([side_high, side_high, side_low, zero], 1).astype(bf16)


def stencil(cells, fraction, live):
    w = [x * live for x in cubic_weights(fraction)]
    d = cell_of(iota((E, STEP), 0)) - (cells - 1)
    return jnp.where(
        d == 0, w[0], jnp.where(d == 1, w[1], jnp.where(d == 2, w[2], jnp.where(d == 3, w[3], 0.0)))
    )


def weights_kernel(points, after, r_high, r_low, r_twice, r_all, c_high, c_low, c_twice):
    kinds = Rows()
    for i in range(points.shape[1] // STEP):
        at = pl.ds(i * STEP, STEP)
        rows, cols, row_fracs, col_fracs, live, _ = fields(points, at)
        r_all[:, at] = stencil(rows, row_fracs, live)
        r_at, r_weights = touched(rows), weight_parts(row_fracs, live)
        r_high[:, at], r_low[:, at] = place(kinds.main, r_at, r_weights)
        r_twice[:, at] = kinds.pair(r_at, r_weights)
        c_at, c_weights = touched(cols), weight_parts(col_fracs)
        c_high[:, at], c_low[:, at] = place(kinds.main, c_at, c_weights)
        c_twice[:, at] = kinds.pair(c_at, c_weights)


def middle_kernel(
    spot, row, group, tail, far, near, yh, yl, scale, scale_tail, points, r_high, r_low, r_twice,
    r_all, c_high, c_low, c_twice, turned, ends, image, main_out, edge_out, far_out, near_out, main, edge,
):
    grid = grid_parts(row, group, tail, far, near, yh, yl, scale, scale_tail)
    kinds = Rows()
    for i in range(points.shape[1] // STEP):
        at = pl.ds(i * STEP, STEP)
        value = pick(grid, (c_high[:, at], c_low[:, at]), c_twice[:, at], r_all[:, at])
        image[:, at] = value
    for i in range(points.shape[1] // STEP):
        at = pl.ds(i * STEP, STEP)
        _, cols, _, col_fracs, _, _ = fields(points, at)
        c_weights = weight_parts(col_fracs, image[:, at])
        r_main = r_high[:, at], r_low[:, at]
        add_spread(i, kinds, r_main, r_twice[:, at], touched(cols), c_weights, main, edge)
    scaled_slabs(
        spot[0] == 0, main[...], edge[...], turned, ends[...], main_out, edge_out, far_out, near_out
    )


def last_kernel(
    row, group, tail, far, near, yh, yl, scale, scale_tail, r_all, c_high, c_low, c_twice, points, image,
    image_two, sums,
):
    grid = grid_parts(row, group, tail, far, near, yh, yl, scale, scale_tail)
    for i in range(r_all.shape[1] // STEP):
        at = pl.ds(i * STEP, STEP)
        image_two[:, at] = pick(grid, (c_high[:, at], c_low[:, at]), c_twice[:, at], r_all[:, at])
    b, v, w = points[5:6], image[...], image_two[...]
    lane = iota((1, 128), 1)
    total = jnp.zeros((1, 128), f32)
    for i, product in enumerate((b * b, b * v, v * v, v * w, w * w)):
        total = jnp.where(lane == i, jnp.sum(product, axis=1, keepdims=True), total)
    sums[...] = jnp.broadcast_to(total, sums.shape)


def finish_kernel(ridge, parts, points, image, image_two, solution_out, residual_out, relative_out):
    total = jnp.sum(parts[...], axis=0, keepdims=True)
    bb, bv, vv, vw, ww = (total[:, i : i + 1] for i in range(5))
    rho = ridge[0]
    b_image = bv + rho * bb
    one = bb / b_image
    keep = 1.0 - one * rho
    mid = keep * keep * bb - 2.0 * keep * one * bv + one * one * vv
    curve = keep * keep * bv - 2.0 * keep * one * vv + one * one * vw
    ratio = mid / bb
    two = mid / (curve + rho * mid - ratio * mid / one)
    side = keep + ratio
    on_b = keep - two * rho * side
    on_v = -one - two * (side - rho * one)
    on_w = two * one
    b, v, w = points[5:6], image[...], image_two[...]
    solution_out[...] = (one + two * side) * b - (two * one) * v
    residual_out[...] = on_b * b + on_v * v + on_w * w
    end = (
        on_b * on_b * bb
        + 2.0 * on_b * on_v * bv
        + (on_v * on_v + 2.0 * on_b * on_w) * vv
        + 2.0 * on_v * on_w * vw
        + on_w * on_w * ww
    )
    relative_out[...] = jnp.broadcast_to(end / bb, relative_out.shape)


def call(kernel, outs, args, scalars=(), scratch=(), mib=20, flops=0):
    vmem = pl.BlockSpec(memory_space=pltpu.VMEM)
    smem = pl.BlockSpec(memory_space=pltpu.SMEM)
    shapes = tuple(jax.ShapeDtypeStruct(shape, dtype) for shape, dtype in outs)
    return pl.pallas_call(
        kernel,
        out_shape=shapes,
        in_specs=[smem if i in scalars else vmem for i in range(len(args))],
        out_specs=tuple(vmem for _ in outs),
        scratch_shapes=list(scratch),
        compiler_params=pltpu.CompilerParams(vmem_limit_bytes=mib << 20),
        cost_estimate=pl.CostEstimate(flops=flops, bytes_accessed=1 << 20, transcendentals=0),
    )(*args)


def solution(mesh):
    gx, gy = mesh.axis_names

    def pairs(axis):
        count = mesh.shape[axis]
        near = [(i, i ^ 1) for i in range(count)]
        far = [(i, (i + 1) % count if i % 2 else (i - 1) % count) for i in range(count)]
        return far, near

    def swap(axis, far, near):
        far_to, near_to = pairs(axis)
        return lax.ppermute(far, axis, far_to), lax.ppermute(near, axis, near_to)

    def shards(row_cells, col_cells, fracs, counts, targets, amplitude, lengthscale, ridge):
        n = targets.shape[2]
        spot = jnp.stack([lax.axis_index(gx) % 2, lax.axis_index(gy) % 2]).astype(jnp.int32)
        vector = ((1, n), f32)
        block = ((T, T), f32)
        main, edge = ((E, T), f32), ((8, 384), f32)
        slab, first_slab = ((SLAB, T), f32), ((SLAB + 16, T), f32)
        strip, corner = ((8, T), f32), ((8, 128), f32)
        row = ((T, 384), f32)
        scales = (main, ((E, 128), f32))
        scratch = (pltpu.VMEM((E, T), f32), pltpu.VMEM((8, 384), f32))

        ends = jnp.concatenate([amplitude[:8], amplitude[T - 8 :]], 0)
        live = (jnp.arange(n) < counts[0, 0]).astype(f32)
        cells = [row_cells[0, 0].astype(f32), col_cells[0, 0].astype(f32)]
        known = [fracs[0, 0, 0], fracs[1, 0, 0], live, targets[0, 0] * live]
        points = jnp.stack(cells + known + [jnp.zeros_like(live)] * 2)
        far_end, near_end = swap(gy, ends, ends)
        bands = call(bands_kernel, (((E, K), bf16),) * 4, (spot, lengthscale), (0, 1))
        x_bands, y_bands = bands[:2], bands[2:]
        half, twice = ((T, n), bf16), ((16, n), bf16)
        inner, rim = call(
            spread_kernel,
            (main, edge),
            (points,),
            flops=6 << 28,
        )
        inner, rim, turned, ends, far, near = call(
            first_slabs_kernel,
            (main, edge, block, strip, first_slab, first_slab),
            (spot, inner, rim, amplitude, far_end, near_end),
            (0,),
        )
        far, near = swap(gx, far, near)
        *across, far, near, outside, ends_corner, scale, scale_tail = call(
            first_across_kernel,
            (row, edge, strip, slab, slab, strip, corner, *scales),
            (spot, inner, rim, amplitude, turned, ends, far, near, *x_bands),
            (0,),
        )
        matrices = call(
            weights_kernel,
            (half, half, twice, ((E, n), f32), half, half, twice),
            (points, ends_corner),
            flops=3 << 28,
        )
        far, near = swap(gy, far, near)
        image, inner, rim, far, near = call(
            middle_kernel,
            (vector, main, edge, slab, slab),
            (
                spot, *across, far, near, *y_bands, scale, scale_tail, points,
                *matrices, turned, ends,
            ),
            (0,),
            scratch,
        )
        far, near = swap(gx, far, near)
        *across, far, near = call(
            across_kernel,
            (row, edge, strip, slab, slab),
            (spot, inner, rim, turned, ends, outside, ends_corner, far, near, *x_bands),
            (0,),
        )
        far, near = swap(gy, far, near)
        devices = mesh.size
        image_two, sums = call(
            last_kernel,
            (vector, ((devices, 128), f32)),
            (*across, far, near, *y_bands, scale, scale_tail, *matrices[3:], points, image),
            (),
        )
        parts = lax.all_to_all(sums.reshape(devices, 1, 128), (gx, gy), 0, 0)
        out, residual, relative = call(
            finish_kernel,
            (vector, vector, ((1, 128), f32)),
            (ridge, parts.reshape(devices, 128), points, image, image_two),
            (0,),
        )
        return out.reshape(1, 1, n), residual.reshape(1, 1, n), relative[0, :1]

    tiles = P(gy, gx, None)
    return jax.shard_map(
        shards,
        mesh=mesh,
        in_specs=(tiles, tiles, P(None, gy, gx, None), P(gy, gx), tiles, P(gy, gx), P(), P()),
        out_specs=(tiles, tiles, P()),
        check_vma=False,
    )
```

```python
import jax
import jax.numpy as jnp
from jax import lax
from jax.experimental import pallas as pl
from jax.experimental.pallas import tpu as pltpu
from jax.sharding import PartitionSpec as P

f32 = jnp.float32
bf16 = jnp.bfloat16
HB = 128
T = 256
HALF = T // 2
E = T + 8
TALL = T + 16
SLAB = HALF + 16
FIELD = 2 * T + 24
K = 2 * T + 128
STEP = 512
MM = (((1,), (0,)), ((), ()))
MT = (((1,), (1,)), ((), ()))


def dot(left, right, dims):
    return lax.dot_general(left, right, dims, preferred_element_type=f32)


def split(x):
    high = x.astype(bf16)
    return high, (x - high.astype(f32)).astype(bf16)


def split_rows(x):
    high = x.astype(bf16).astype(f32)
    return jnp.concatenate([high, x - high], 0).astype(bf16)


def iota(shape, dim):
    return lax.broadcasted_iota(jnp.int32, shape, dim)


def cell_of(slot):
    return jnp.where(slot <= T + 1, slot, jnp.where(slot == T + 2, -1, -9999))


def cubic_weights(fraction):
    square = fraction * fraction
    cube = square * fraction
    return (
        -0.5 * cube + square - 0.5 * fraction,
        1.5 * cube - 2.5 * square + 1.0,
        -1.5 * cube + 2.0 * square + 0.5 * fraction,
        0.5 * cube - 0.5 * square,
    )


def slots(first, count, wrap):
    cell = cell_of(first + iota((count, 128), 0) % wrap).astype(jnp.int16)
    return jnp.concatenate([cell] * (STEP // 128), 1)


def place(cell, targets, weights):
    hits = [cell == target for target in targets]
    out = []
    for group in weights:
        value = jnp.zeros(cell.shape, bf16)
        for hit, weight in zip(hits, group):
            value = jnp.where(hit, jnp.broadcast_to(weight, cell.shape), value)
        out.append(value)
    return out


def touched(cells):
    return [(cells + (j - 1)).astype(jnp.int16) for j in range(4)]


def weight_parts(fraction, factor=None):
    pairs = [split(w if factor is None else w * factor) for w in cubic_weights(fraction)]
    return [high for high, _ in pairs], [low for _, low in pairs]


class Rows:
    def __init__(self):
        self.main = slots(0, T, T)
        self.tail = slots(T, 16, 16)
        self.twice = slots(T, 16, 8)
        self.upper = iota((16, STEP), 0) < 8

    def pair(self, targets, weights):
        high, low = place(self.twice, targets, weights)
        return jnp.where(self.upper, high.astype(f32), low.astype(f32)).astype(bf16)


def add_spread(i, rows, r_main, r_pair, targets, weights, out, edge):
    main, tail = place(rows.main, targets, weights), place(rows.tail, targets, weights)
    high, low = (jnp.concatenate([x, y], 0) for x, y in zip(main, tail))
    inner = dot(high, r_main[0], MT) + dot(high, r_main[1], MT) + dot(low, r_main[0], MT)
    first = dot(r_pair, high, MT)
    side = first[:8] + first[8:] + dot(r_pair, low, MT)[:8]
    if i == 0:
        edge[...] = jnp.zeros_like(edge)
        out[...] = inner[:E]
        edge[:, :TALL] = side
    else:
        out[...] += inner[:E]
        edge[:, :TALL] += side


def pick(grid, c_main, c_pair, r):
    high, low, tails = grid
    value = dot(high, c_main[0], MM) + dot(high, c_main[1], MM) + dot(low, c_main[0], MM)
    out = jnp.sum(value * r, axis=0, keepdims=True)
    c_tail = c_pair.astype(f32)
    for i, tail in enumerate(tails):
        across = jnp.sum(jnp.concatenate([tail] * (STEP // 128), 1) * r, axis=0, keepdims=True)
        out = out + across * (c_tail[i : i + 1] + c_tail[8 + i : 9 + i])
    return out


def put(row, value, index, x):
    return jnp.where(row == index, jnp.broadcast_to(value, x.shape), x)


def group_low(x, tail, dim):
    row = iota(tail.shape, dim)
    at = (lambda i: x[i : i + 1]) if dim == 0 else (lambda i: x[:, i : i + 1])
    return put(row, at(HALF), 6, put(row, at(HALF + 1), 7, tail))


def group_high(x, tail, dim):
    row = iota(tail.shape, dim)
    at = (lambda i: x[i : i + 1]) if dim == 0 else (lambda i: x[:, i : i + 1])
    return put(row, at(HALF - 1), 7, tail)


def edge_rows(x):
    row = iota((8, x.shape[1]), 0)
    return jnp.where(row < 2, x[:8], jnp.broadcast_to(x[T - 1 : T], row.shape))


def outside_rows(even, far, near):
    row = iota(far.shape, 0)
    before = jnp.where(even, far, near)
    after = jnp.where(even, near, far)
    return jnp.where(row < 2, after, jnp.where(row == 2, before, 0.0))


def outside_lanes(even, far, near):
    lane = iota((8, 128), 1)
    before = jnp.where(even, far, near)
    after = jnp.where(even, near, far)
    last = jnp.broadcast_to(before[:, T - 1 : T], lane.shape)
    return jnp.where(lane < 2, after[:, :128], jnp.where(lane == 2, last, 0.0))


def column_slabs(even, main, edge, far, near):
    tail = main[T:]
    low_rows, high_rows = group_low(main, tail, 0), group_high(main, tail, 0)
    lanes = edge[:, T:]
    low_lanes, high_lanes = group_low(edge, lanes, 1), group_high(edge, lanes, 1)
    for ref, low, shift in ((far, even, 8), (near, jnp.logical_not(even), 16)):
        ref[:HALF] = jnp.where(low, main[:HALF], main[HALF:T])
        ref[HALF : HALF + 8] = jnp.where(low, low_rows, high_rows)
        ref[HALF + 8 : SLAB, :128] = jnp.where(low, edge[:, :HALF], edge[:, HALF:T])
        group = jnp.where(low, low_lanes, high_lanes)
        group = jnp.where(iota(group.shape, 1) < 8, group, 0.0)
        ref[HALF + 8 : SLAB, 128:] = pltpu.roll(group, shift, 1)


def row_slabs(even, main, group, tail, far, near):
    low_rows, high_rows = group_low(main, group, 0), group_high(main, group, 0)
    for ref, low in ((far, even), (near, jnp.logical_not(even))):
        ref[:HALF] = jnp.where(low, main[:HALF, :T], main[HALF:, :T])
        rows = jnp.where(low, low_rows, high_rows)
        ref[HALF : HALF + 8] = rows[:, :T]
        ref[HALF + 8 : SLAB, :128] = jnp.where(low, tail[:, :HALF], tail[:, HALF:])
        ref[HALF + 8 : SLAB, 128:] = rows[:, T:]


def smooth_by(bands, x):
    high, low = split(x)
    return dot(bands[0], high, MM) + dot(bands[0], low, MM) + dot(bands[1], high, MM)


def band(even, scale, high, low):
    out = cell_of(iota((E, K), 0))
    k = iota((E, K), 1)
    j = k - 2 * T
    is_own = jnp.logical_or(k < T, jnp.logical_and(j >= 0, j < 8))
    is_far = jnp.logical_or(
        jnp.logical_and(k >= T, k < T + HALF), jnp.logical_and(j >= 8, j < 16)
    )
    before = is_far == even
    g = j % 8
    extra = jnp.where(before, jnp.where(g == 7, HALF - 1, -9999), g + (HALF - 6))
    extra = jnp.where(jnp.logical_or(is_own, g < 6), -9999, extra)
    group = jnp.where(g < 3, cell_of(T + g), extra)
    inner = jnp.where(is_own, k, k % HALF + jnp.where(before, HALF, 0))
    cell = jnp.where(j < 0, inner, jnp.where(j < 24, group, -9999))
    source = jnp.where(is_own, cell, jnp.where(before, cell - T, cell + T))
    d = jnp.abs(source - out)
    distance = d.astype(f32)
    value = jnp.where(
        jnp.logical_and(d <= HB, out >= -1),
        jnp.exp(-distance * distance / (2.0 * scale * scale)),
        0.0,
    )
    high[...], low[...] = split(value)


def bands_kernel(spot, scales, xh, xl, yh, yl):
    band(spot[0] == 0, scales[1], xh, xl)
    band(spot[1] == 0, scales[0], yh, yl)


def fields(points, at):
    cells = [points[i : i + 1, at].astype(jnp.int32) for i in range(2)]
    return cells + [points[i : i + 1, at] for i in range(2, 6)]


def spread_kernel(points, out, edge):
    kinds = Rows()
    for i in range(points.shape[1] // STEP):
        at = pl.ds(i * STEP, STEP)
        rows, cols, row_fracs, col_fracs, live, vector = fields(points, at)
        r_at, r_weights = touched(rows), weight_parts(row_fracs, live)
        r_main = place(kinds.main, r_at, r_weights)
        r_pair = kinds.pair(r_at, r_weights)
        c_weights = weight_parts(col_fracs, vector)
        add_spread(i, kinds, r_main, r_pair, touched(cols), c_weights, out, edge)


def scaled_slabs(even, main, edge, turned, ends, main_out, edge_out, far, near):
    main_out[:T] = main[:T] * turned[...]
    main_out[T:] = main[T:]
    edge_out[:, :T] = edge[:, :T] * ends
    edge_out[:, T:] = edge[:, T:]
    column_slabs(even, main_out[...], edge_out[...], far, near)


def first_slabs_kernel(
    spot, main, edge, amplitude, far_ends, near_ends, main_out, edge_out, turned, ends, far, near
):
    row = iota((8, T), 0)
    far_rows, near_rows = (
        jnp.where(row < 2, x[:8], jnp.broadcast_to(x[15:], row.shape)) for x in (far_ends, near_ends)
    )
    ends[...] = outside_rows(spot[1] == 0, far_rows, near_rows)
    turned[...] = jnp.transpose(amplitude[...])
    scaled_slabs(
        spot[0] == 0, main[...], edge[...], turned, ends[...], main_out, edge_out, far, near
    )
    for ref in (far, near):
        ref[SLAB : SLAB + 8] = edge_rows(turned[...])
        ref[SLAB + 8 :] = ends[...]


def across_body(even_row, main, edge, turned, ends, outside, corner, far, near, bands, outs):
    row_out, group_out, tail_out, far_out, near_out = outs
    row = iota((8, T), 0)
    edges = jnp.where(row < 3, edge_rows(turned), 1.0)
    field = jnp.concatenate(
        [
            main[:T],
            far[:HALF],
            near[:HALF],
            main[T:] * outside,
            far[HALF : HALF + 8] * edges,
            near[HALF : HALF + 8] * edges,
        ],
        0,
    )
    smoothed = smooth_by((bands[0][:, :FIELD], bands[1][:, :FIELD]), field)
    lane = iota((8, 128), 1)
    g = lane % 8
    first, second = (jnp.broadcast_to(ends[:, i : i + 1], lane.shape) for i in (0, 1))
    third = jnp.broadcast_to(ends[:, T - 1 : T], lane.shape)
    factor = jnp.where(g == 0, first, jnp.where(g == 1, second, jnp.where(g == 2, third, 1.0)))
    factor = jnp.where(lane < 8, corner, factor)
    own = jnp.where(lane < 8, edge[:, T:], 0.0)
    groups = (own + far[HALF + 8 : SLAB, 128:] + near[HALF + 8 : SLAB, 128:]) * factor
    strip = jnp.concatenate(
        [edge[:, :T], far[HALF + 8 : SLAB, :128], near[HALF + 8 : SLAB, :128], groups], 1
    )
    pair = split_rows(strip)
    by_high = dot(pair, bands[0], MT)
    group = by_high[:8] + by_high[8:] + dot(pair, bands[1], MT)[:8]
    group = jnp.concatenate([group, jnp.zeros((8, 384 - E), f32)], 1)
    turned_back = jnp.transpose(jnp.concatenate([smoothed, jnp.zeros((384 - E, T), f32)], 0))
    row_out[...] = turned_back
    group_out[...] = group
    tail_out[...] = smoothed[T:]
    row_slabs(even_row, turned_back, group, smoothed[T:], far_out, near_out)


def first_across_kernel(
    spot, main, edge, amplitude, turned, ends, far, near, xh, xl,
    row_out, group_out, tail_out, far_out, near_out, outside, corner, scale, scale_tail,
):
    even = spot[0] == 0
    outside[...] = outside_rows(even, far[SLAB : SLAB + 8], near[SLAB : SLAB + 8])
    corner[...] = outside_lanes(even, far[SLAB + 8 :], near[SLAB + 8 :])
    scale[:T] = amplitude[...]
    scale[T:] = ends[...]
    wide = jnp.concatenate([outside[...], jnp.zeros((120, T), f32)], 0)
    scale_tail[:T] = jnp.transpose(wide)
    scale_tail[T:] = corner[...]
    across_body(
        spot[1] == 0, main[...], edge[...], turned[...], ends[...], outside[...], corner[...],
        far[...], near[...], (xh[...], xl[...]), (row_out, group_out, tail_out, far_out, near_out),
    )


def across_kernel(
    spot, main, edge, turned, ends, outside, corner, far, near, xh, xl,
    row_out, group_out, tail_out, far_out, near_out,
):
    across_body(
        spot[1] == 0, main[...], edge[...], turned[...], ends[...], outside[...], corner[...],
        far[...], near[...], (xh[...], xl[...]), (row_out, group_out, tail_out, far_out, near_out),
    )


def grid_parts(row, group, tail, far, near, yh, yl, scale, scale_tail):
    far_group, near_group = far[HALF : HALF + 8], near[HALF : HALF + 8]
    field = jnp.concatenate(
        [row[:, :T], far[:HALF], near[:HALF], group[:, :T], far_group, near_group], 0
    )
    main = smooth_by((yh[:, :FIELD], yl[:, :FIELD]), field) * scale[...]
    strip = jnp.concatenate(
        [tail[...], far[HALF + 8 : SLAB, :128], near[HALF + 8 : SLAB, :128]], 1
    )
    pair = split_rows(strip)
    by_high = dot(yh[:, : 2 * T], pair, MT)
    side = by_high[:, :8] + by_high[:, 8:] + dot(yl[:, : 2 * T], pair, MT)[:, :8]
    ends = jnp.concatenate(
        [group[:, T:], far[HALF + 8 : SLAB, 128:], near[HALF + 8 : SLAB, 128:]], 0
    )
    side = side + smooth_by((yh[:, 2 * T : FIELD], yl[:, 2 * T : FIELD]), ends)[:, :8]
    side = side * scale_tail[:, :8]
    high, low = split(main)
    return high, low, [jnp.broadcast_to(side[:, i : i + 1], (E, 128)) for i in range(3)]


def stencil(cells, fraction, live):
    w = [x * live for x in cubic_weights(fraction)]
    d = cell_of(iota((E, STEP), 0)) - (cells - 1)
    return jnp.where(
        d == 0, w[0], jnp.where(d == 1, w[1], jnp.where(d == 2, w[2], jnp.where(d == 3, w[3], 0.0)))
    )


def weights_kernel(points, after, r_high, r_low, r_twice, r_all, c_high, c_low, c_twice):
    kinds = Rows()
    for i in range(points.shape[1] // STEP):
        at = pl.ds(i * STEP, STEP)
        rows, cols, row_fracs, col_fracs, live, _ = fields(points, at)
        r_all[:, at] = stencil(rows, row_fracs, live)
        r_at, r_weights = touched(rows), weight_parts(row_fracs, live)
        r_high[:, at], r_low[:, at] = place(kinds.main, r_at, r_weights)
        r_twice[:, at] = kinds.pair(r_at, r_weights)
        c_at, c_weights = touched(cols), weight_parts(col_fracs)
        c_high[:, at], c_low[:, at] = place(kinds.main, c_at, c_weights)
        c_twice[:, at] = kinds.pair(c_at, c_weights)


def middle_kernel(
    spot, row, group, tail, far, near, yh, yl, scale, scale_tail, points, r_high, r_low, r_twice,
    r_all, c_high, c_low, c_twice, turned, ends, image, main_out, edge_out, far_out, near_out, main, edge,
):
    grid = grid_parts(row, group, tail, far, near, yh, yl, scale, scale_tail)
    kinds = Rows()
    for i in range(points.shape[1] // STEP):
        at = pl.ds(i * STEP, STEP)
        value = pick(grid, (c_high[:, at], c_low[:, at]), c_twice[:, at], r_all[:, at])
        image[:, at] = value
    for i in range(points.shape[1] // STEP):
        at = pl.ds(i * STEP, STEP)
        _, cols, _, col_fracs, _, _ = fields(points, at)
        c_weights = weight_parts(col_fracs, image[:, at])
        r_main = r_high[:, at], r_low[:, at]
        add_spread(i, kinds, r_main, r_twice[:, at], touched(cols), c_weights, main, edge)
    scaled_slabs(
        spot[0] == 0, main[...], edge[...], turned, ends[...], main_out, edge_out, far_out, near_out
    )


def last_kernel(
    row, group, tail, far, near, yh, yl, scale, scale_tail, r_all, c_high, c_low, c_twice, points, image,
    image_two, sums,
):
    grid = grid_parts(row, group, tail, far, near, yh, yl, scale, scale_tail)
    for i in range(r_all.shape[1] // STEP):
        at = pl.ds(i * STEP, STEP)
        image_two[:, at] = pick(grid, (c_high[:, at], c_low[:, at]), c_twice[:, at], r_all[:, at])
    b, v, w = points[5:6], image[...], image_two[...]
    lane = iota((1, 128), 1)
    total = jnp.zeros((1, 128), f32)
    for i, product in enumerate((b * b, b * v, v * v, v * w, w * w)):
        total = jnp.where(lane == i, jnp.sum(product, axis=1, keepdims=True), total)
    sums[...] = jnp.broadcast_to(total, sums.shape)


def finish_kernel(ridge, parts, points, image, image_two, solution_out, residual_out, relative_out):
    total = jnp.sum(parts[...], axis=0, keepdims=True)
    bb, bv, vv, vw, ww = (total[:, i : i + 1] for i in range(5))
    rho = ridge[0]
    b_image = bv + rho * bb
    one = bb / b_image
    keep = 1.0 - one * rho
    mid = keep * keep * bb - 2.0 * keep * one * bv + one * one * vv
    curve = keep * keep * bv - 2.0 * keep * one * vv + one * one * vw
    ratio = mid / bb
    two = mid / (curve + rho * mid - ratio * mid / one)
    side = keep + ratio
    on_b = keep - two * rho * side
    on_v = -one - two * (side - rho * one)
    on_w = two * one
    b, v, w = points[5:6], image[...], image_two[...]
    solution_out[...] = (one + two * side) * b - (two * one) * v
    residual_out[...] = on_b * b + on_v * v + on_w * w
    end = (
        on_b * on_b * bb
        + 2.0 * on_b * on_v * bv
        + (on_v * on_v + 2.0 * on_b * on_w) * vv
        + 2.0 * on_v * on_w * vw
        + on_w * on_w * ww
    )
    relative_out[...] = jnp.broadcast_to(end / bb, relative_out.shape)


def call(kernel, outs, args, scalars=(), scratch=(), mib=20, flops=0):
    vmem = pl.BlockSpec(memory_space=pltpu.VMEM)
    smem = pl.BlockSpec(memory_space=pltpu.SMEM)
    shapes = tuple(jax.ShapeDtypeStruct(shape, dtype) for shape, dtype in outs)
    return pl.pallas_call(
        kernel,
        out_shape=shapes,
        in_specs=[smem if i in scalars else vmem for i in range(len(args))],
        out_specs=tuple(vmem for _ in outs),
        scratch_shapes=list(scratch),
        compiler_params=pltpu.CompilerParams(vmem_limit_bytes=mib << 20),
        cost_estimate=pl.CostEstimate(flops=flops, bytes_accessed=1 << 20, transcendentals=0),
    )(*args)


def solution(mesh):
    gx, gy = mesh.axis_names

    def pairs(axis):
        count = mesh.shape[axis]
        near = [(i, i ^ 1) for i in range(count)]
        far = [(i, (i + 1) % count if i % 2 else (i - 1) % count) for i in range(count)]
        return far, near

    def swap(axis, far, near):
        far_to, near_to = pairs(axis)
        near = lax.ppermute(near, axis, near_to)
        far = lax.ppermute(far, axis, far_to)
        return far, near

    def shards(row_cells, col_cells, fracs, counts, targets, amplitude, lengthscale, ridge):
        n = targets.shape[2]
        spot = jnp.stack([lax.axis_index(gx) % 2, lax.axis_index(gy) % 2]).astype(jnp.int32)
        vector = ((1, n), f32)
        block = ((T, T), f32)
        main, edge = ((E, T), f32), ((8, 384), f32)
        slab, first_slab = ((SLAB, T), f32), ((SLAB + 16, T), f32)
        strip, corner = ((8, T), f32), ((8, 128), f32)
        row = ((T, 384), f32)
        scales = (main, ((E, 128), f32))
        scratch = (pltpu.VMEM((E, T), f32), pltpu.VMEM((8, 384), f32))

        ends = jnp.concatenate([amplitude[:8], amplitude[T - 8 :]], 0)
        live = (jnp.arange(n) < counts[0, 0]).astype(f32)
        cells = [row_cells[0, 0].astype(f32), col_cells[0, 0].astype(f32)]
        known = [fracs[0, 0, 0], fracs[1, 0, 0], live, targets[0, 0] * live]
        points = jnp.stack(cells + known + [jnp.zeros_like(live)] * 2)
        far_end, near_end = swap(gy, ends, ends)
        bands = call(bands_kernel, (((E, K), bf16),) * 4, (spot, lengthscale), (0, 1))
        x_bands, y_bands = bands[:2], bands[2:]
        half, twice = ((T, n), bf16), ((16, n), bf16)
        inner, rim = call(
            spread_kernel,
            (main, edge),
            (points,),
            flops=6 << 28,
        )
        inner, rim, turned, ends, far, near = call(
            first_slabs_kernel,
            (main, edge, block, strip, first_slab, first_slab),
            (spot, inner, rim, amplitude, far_end, near_end),
            (0,),
        )
        far, near = swap(gx, far, near)
        *across, far, near, outside, ends_corner, scale, scale_tail = call(
            first_across_kernel,
            (row, edge, strip, slab, slab, strip, corner, *scales),
            (spot, inner, rim, amplitude, turned, ends, far, near, *x_bands),
            (0,),
        )
        matrices = call(
            weights_kernel,
            (half, half, twice, ((E, n), f32), half, half, twice),
            (points, ends_corner),
            flops=3 << 28,
        )
        far, near = swap(gy, far, near)
        image, inner, rim, far, near = call(
            middle_kernel,
            (vector, main, edge, slab, slab),
            (
                spot, *across, far, near, *y_bands, scale, scale_tail, points,
                *matrices, turned, ends,
            ),
            (0,),
            scratch,
        )
        far, near = swap(gx, far, near)
        *across, far, near = call(
            across_kernel,
            (row, edge, strip, slab, slab),
            (spot, inner, rim, turned, ends, outside, ends_corner, far, near, *x_bands),
            (0,),
        )
        far, near = swap(gy, far, near)
        devices = mesh.size
        image_two, sums = call(
            last_kernel,
            (vector, ((devices, 128), f32)),
            (*across, far, near, *y_bands, scale, scale_tail, *matrices[3:], points, image),
            (),
        )
        parts = lax.all_to_all(sums.reshape(devices, 1, 128), (gx, gy), 0, 0)
        out, residual, relative = call(
            finish_kernel,
            (vector, vector, ((1, 128), f32)),
            (ridge, parts.reshape(devices, 128), points, image, image_two),
            (0,),
        )
        return out.reshape(1, 1, n), residual.reshape(1, 1, n), relative[0, :1]

    tiles = P(gy, gx, None)
    return jax.shard_map(
        shards,
        mesh=mesh,
        in_specs=(tiles, tiles, P(None, gy, gx, None), P(gy, gx), tiles, P(gy, gx), P(), P()),
        out_specs=(tiles, tiles, P()),
        check_vma=False,
    )
```

```python
import jax
import jax.numpy as jnp
from jax import lax
from jax.experimental import pallas as pl
from jax.experimental.pallas import tpu as pltpu
from jax.sharding import PartitionSpec as P

f32 = jnp.float32
bf16 = jnp.bfloat16
HB = 128
T = 256
HALF = T // 2
E = T + 8
TALL = T + 16
SLAB = HALF + 16
FIELD = 2 * T + 24
K = 2 * T + 128
STEP = 512
MM = (((1,), (0,)), ((), ()))
MT = (((1,), (1,)), ((), ()))


def dot(left, right, dims):
    return lax.dot_general(left, right, dims, preferred_element_type=f32)


def split(x):
    high = x.astype(bf16)
    return high, (x - high.astype(f32)).astype(bf16)


def split_rows(x):
    high = x.astype(bf16).astype(f32)
    return jnp.concatenate([high, x - high], 0).astype(bf16)


def iota(shape, dim):
    return lax.broadcasted_iota(jnp.int32, shape, dim)


def cell_of(slot):
    return jnp.where(slot <= T + 1, slot, jnp.where(slot == T + 2, -1, -9999))


def cubic_weights(fraction):
    square = fraction * fraction
    cube = square * fraction
    return (
        -0.5 * cube + square - 0.5 * fraction,
        1.5 * cube - 2.5 * square + 1.0,
        -1.5 * cube + 2.0 * square + 0.5 * fraction,
        0.5 * cube - 0.5 * square,
    )


def slots(first, count, wrap):
    cell = cell_of(first + iota((count, 128), 0) % wrap).astype(jnp.int16)
    return jnp.concatenate([cell] * (STEP // 128), 1)


def place(cell, targets, weights):
    hits = [cell == target for target in targets]
    out = []
    for group in weights:
        value = jnp.zeros(cell.shape, bf16)
        for hit, weight in zip(hits, group):
            value = jnp.where(hit, jnp.broadcast_to(weight, cell.shape), value)
        out.append(value)
    return out


def touched(cells):
    return [(cells + (j - 1)).astype(jnp.int16) for j in range(4)]


def weight_parts(fraction, factor=None):
    pairs = [split(w if factor is None else w * factor) for w in cubic_weights(fraction)]
    return [high for high, _ in pairs], [low for _, low in pairs]


class Rows:
    def __init__(self):
        self.main = slots(0, T, T)
        self.tail = slots(T, 16, 16)
        self.twice = slots(T, 16, 8)
        self.upper = iota((16, STEP), 0) < 8

    def pair(self, targets, weights):
        high, low = place(self.twice, targets, weights)
        return jnp.where(self.upper, high.astype(f32), low.astype(f32)).astype(bf16)


def add_spread(i, rows, r_main, r_pair, targets, weights, out, edge):
    main, tail = place(rows.main, targets, weights), place(rows.tail, targets, weights)
    high, low = (jnp.concatenate([x, y], 0) for x, y in zip(main, tail))
    inner = dot(high, r_main[0], MT) + dot(high, r_main[1], MT) + dot(low, r_main[0], MT)
    first = dot(r_pair, high, MT)
    side = first[:8] + first[8:] + dot(r_pair, low, MT)[:8]
    if i == 0:
        edge[...] = jnp.zeros_like(edge)
        out[...] = inner[:E]
        edge[:, :TALL] = side
    else:
        out[...] += inner[:E]
        edge[:, :TALL] += side


def pick(grid, c_main, c_pair, r):
    high, low, tails = grid
    value = dot(high, c_main[0], MM) + dot(high, c_main[1], MM) + dot(low, c_main[0], MM)
    out = jnp.sum(value * r, axis=0, keepdims=True)
    c_tail = c_pair.astype(f32)
    for i, tail in enumerate(tails):
        across = jnp.sum(jnp.concatenate([tail] * (STEP // 128), 1) * r, axis=0, keepdims=True)
        out = out + across * (c_tail[i : i + 1] + c_tail[8 + i : 9 + i])
    return out


def put(row, value, index, x):
    return jnp.where(row == index, jnp.broadcast_to(value, x.shape), x)


def group_low(x, tail, dim):
    row = iota(tail.shape, dim)
    at = (lambda i: x[i : i + 1]) if dim == 0 else (lambda i: x[:, i : i + 1])
    return put(row, at(HALF), 6, put(row, at(HALF + 1), 7, tail))


def group_high(x, tail, dim):
    row = iota(tail.shape, dim)
    at = (lambda i: x[i : i + 1]) if dim == 0 else (lambda i: x[:, i : i + 1])
    return put(row, at(HALF - 1), 7, tail)


def edge_rows(x):
    row = iota((8, x.shape[1]), 0)
    return jnp.where(row < 2, x[:8], jnp.broadcast_to(x[T - 1 : T], row.shape))


def outside_rows(even, far, near):
    row = iota(far.shape, 0)
    before = jnp.where(even, far, near)
    after = jnp.where(even, near, far)
    return jnp.where(row < 2, after, jnp.where(row == 2, before, 0.0))


def outside_lanes(even, far, near):
    lane = iota((8, 128), 1)
    before = jnp.where(even, far, near)
    after = jnp.where(even, near, far)
    last = jnp.broadcast_to(before[:, T - 1 : T], lane.shape)
    return jnp.where(lane < 2, after[:, :128], jnp.where(lane == 2, last, 0.0))


def column_slabs(even, main, edge, far, near):
    tail = main[T:]
    low_rows, high_rows = group_low(main, tail, 0), group_high(main, tail, 0)
    lanes = edge[:, T:]
    low_lanes, high_lanes = group_low(edge, lanes, 1), group_high(edge, lanes, 1)
    for ref, low, shift in ((far, even, 8), (near, jnp.logical_not(even), 16)):
        ref[:HALF] = jnp.where(low, main[:HALF], main[HALF:T])
        ref[HALF : HALF + 8] = jnp.where(low, low_rows, high_rows)
        ref[HALF + 8 : SLAB, :128] = jnp.where(low, edge[:, :HALF], edge[:, HALF:T])
        group = jnp.where(low, low_lanes, high_lanes)
        group = jnp.where(iota(group.shape, 1) < 8, group, 0.0)
        ref[HALF + 8 : SLAB, 128:] = pltpu.roll(group, shift, 1)


def row_slabs(even, main, group, tail, far, near):
    low_rows, high_rows = group_low(main, group, 0), group_high(main, group, 0)
    for ref, low in ((far, even), (near, jnp.logical_not(even))):
        ref[:HALF] = jnp.where(low, main[:HALF, :T], main[HALF:, :T])
        rows = jnp.where(low, low_rows, high_rows)
        ref[HALF : HALF + 8] = rows[:, :T]
        ref[HALF + 8 : SLAB, :128] = jnp.where(low, tail[:, :HALF], tail[:, HALF:])
        ref[HALF + 8 : SLAB, 128:] = rows[:, T:]


def smooth_by(bands, x):
    high, low = split(x)
    return dot(bands[0], high, MM) + dot(bands[0], low, MM) + dot(bands[1], high, MM)


def band(even, scale, high, low):
    out = cell_of(iota((E, K), 0))
    k = iota((E, K), 1)
    j = k - 2 * T
    is_own = jnp.logical_or(k < T, jnp.logical_and(j >= 0, j < 8))
    is_far = jnp.logical_or(
        jnp.logical_and(k >= T, k < T + HALF), jnp.logical_and(j >= 8, j < 16)
    )
    before = is_far == even
    g = j % 8
    extra = jnp.where(before, jnp.where(g == 7, HALF - 1, -9999), g + (HALF - 6))
    extra = jnp.where(jnp.logical_or(is_own, g < 6), -9999, extra)
    group = jnp.where(g < 3, cell_of(T + g), extra)
    inner = jnp.where(is_own, k, k % HALF + jnp.where(before, HALF, 0))
    cell = jnp.where(j < 0, inner, jnp.where(j < 24, group, -9999))
    source = jnp.where(is_own, cell, jnp.where(before, cell - T, cell + T))
    d = jnp.abs(source - out)
    distance = d.astype(f32)
    value = jnp.where(
        jnp.logical_and(d <= HB, out >= -1),
        jnp.exp(-distance * distance / (2.0 * scale * scale)),
        0.0,
    )
    high[...], low[...] = split(value)


def bands_kernel(spot, scales, xh, xl, yh, yl):
    band(spot[0] == 0, scales[1], xh, xl)
    band(spot[1] == 0, scales[0], yh, yl)


def fields(points, at):
    cells = [points[i : i + 1, at].astype(jnp.int32) for i in range(2)]
    return cells + [points[i : i + 1, at] for i in range(2, 6)]


def spread_kernel(points, out, edge):
    kinds = Rows()
    for i in range(points.shape[1] // STEP):
        at = pl.ds(i * STEP, STEP)
        rows, cols, row_fracs, col_fracs, live, vector = fields(points, at)
        r_at, r_weights = touched(rows), weight_parts(row_fracs, live)
        r_main = place(kinds.main, r_at, r_weights)
        r_pair = kinds.pair(r_at, r_weights)
        c_weights = weight_parts(col_fracs, vector)
        add_spread(i, kinds, r_main, r_pair, touched(cols), c_weights, out, edge)


def scaled_slabs(even, main, edge, turned, ends, main_out, edge_out, far, near):
    main_out[:T] = main[:T] * turned[...]
    main_out[T:] = main[T:]
    edge_out[:, :T] = edge[:, :T] * ends
    edge_out[:, T:] = edge[:, T:]
    column_slabs(even, main_out[...], edge_out[...], far, near)


def first_slabs_kernel(
    spot, main, edge, amplitude, far_ends, near_ends, main_out, edge_out, turned, ends, far, near
):
    row = iota((8, T), 0)
    far_rows, near_rows = (
        jnp.where(row < 2, x[:8], jnp.broadcast_to(x[15:], row.shape)) for x in (far_ends, near_ends)
    )
    ends[...] = outside_rows(spot[1] == 0, far_rows, near_rows)
    turned[...] = jnp.transpose(amplitude[...])
    scaled_slabs(
        spot[0] == 0, main[...], edge[...], turned, ends[...], main_out, edge_out, far, near
    )
    for ref in (far, near):
        ref[SLAB : SLAB + 8] = edge_rows(turned[...])
        ref[SLAB + 8 :] = ends[...]


def across_body(even_row, main, edge, turned, ends, outside, corner, far, near, bands, outs):
    row_out, group_out, tail_out, far_out, near_out = outs
    row = iota((8, T), 0)
    edges = jnp.where(row < 3, edge_rows(turned), 1.0)
    field = jnp.concatenate(
        [
            main[:T],
            far[:HALF],
            near[:HALF],
            main[T:] * outside,
            far[HALF : HALF + 8] * edges,
            near[HALF : HALF + 8] * edges,
        ],
        0,
    )
    smoothed = smooth_by((bands[0][:, :FIELD], bands[1][:, :FIELD]), field)
    lane = iota((8, 128), 1)
    g = lane % 8
    first, second = (jnp.broadcast_to(ends[:, i : i + 1], lane.shape) for i in (0, 1))
    third = jnp.broadcast_to(ends[:, T - 1 : T], lane.shape)
    factor = jnp.where(g == 0, first, jnp.where(g == 1, second, jnp.where(g == 2, third, 1.0)))
    factor = jnp.where(lane < 8, corner, factor)
    own = jnp.where(lane < 8, edge[:, T:], 0.0)
    groups = (own + far[HALF + 8 : SLAB, 128:] + near[HALF + 8 : SLAB, 128:]) * factor
    strip = jnp.concatenate(
        [edge[:, :T], far[HALF + 8 : SLAB, :128], near[HALF + 8 : SLAB, :128], groups], 1
    )
    pair = split_rows(strip)
    by_high = dot(pair, bands[0], MT)
    group = by_high[:8] + by_high[8:] + dot(pair, bands[1], MT)[:8]
    group = jnp.concatenate([group, jnp.zeros((8, 384 - E), f32)], 1)
    turned_back = jnp.transpose(jnp.concatenate([smoothed, jnp.zeros((384 - E, T), f32)], 0))
    row_out[...] = turned_back
    group_out[...] = group
    tail_out[...] = smoothed[T:]
    row_slabs(even_row, turned_back, group, smoothed[T:], far_out, near_out)


def first_across_kernel(
    spot, main, edge, amplitude, turned, ends, far, near, xh, xl,
    row_out, group_out, tail_out, far_out, near_out, outside, corner, scale, scale_tail,
):
    even = spot[0] == 0
    outside[...] = outside_rows(even, far[SLAB : SLAB + 8], near[SLAB : SLAB + 8])
    corner[...] = outside_lanes(even, far[SLAB + 8 :], near[SLAB + 8 :])
    scale[:T] = amplitude[...]
    scale[T:] = ends[...]
    wide = jnp.concatenate([outside[...], jnp.zeros((120, T), f32)], 0)
    scale_tail[:T] = jnp.transpose(wide)
    scale_tail[T:] = corner[...]
    across_body(
        spot[1] == 0, main[...], edge[...], turned[...], ends[...], outside[...], corner[...],
        far[...], near[...], (xh[...], xl[...]), (row_out, group_out, tail_out, far_out, near_out),
    )


def across_kernel(
    spot, main, edge, turned, ends, outside, corner, far, near, xh, xl,
    row_out, group_out, tail_out, far_out, near_out,
):
    across_body(
        spot[1] == 0, main[...], edge[...], turned[...], ends[...], outside[...], corner[...],
        far[...], near[...], (xh[...], xl[...]), (row_out, group_out, tail_out, far_out, near_out),
    )


def grid_parts(row, group, tail, far, near, yh, yl, scale, scale_tail):
    far_group, near_group = far[HALF : HALF + 8], near[HALF : HALF + 8]
    field = jnp.concatenate(
        [row[:, :T], far[:HALF], near[:HALF], group[:, :T], far_group, near_group], 0
    )
    main = smooth_by((yh[:, :FIELD], yl[:, :FIELD]), field) * scale[...]
    strip = jnp.concatenate(
        [tail[...], far[HALF + 8 : SLAB, :128], near[HALF + 8 : SLAB, :128]], 1
    )
    pair = split_rows(strip)
    by_high = dot(yh[:, : 2 * T], pair, MT)
    side = by_high[:, :8] + by_high[:, 8:] + dot(yl[:, : 2 * T], pair, MT)[:, :8]
    ends = jnp.concatenate(
        [group[:, T:], far[HALF + 8 : SLAB, 128:], near[HALF + 8 : SLAB, 128:]], 0
    )
    side = side + smooth_by((yh[:, 2 * T : FIELD], yl[:, 2 * T : FIELD]), ends)[:, :8]
    side = side * scale_tail[:, :8]
    high, low = split(main)
    return high, low, [jnp.broadcast_to(side[:, i : i + 1], (E, 128)) for i in range(3)]


def stencil(cells, fraction, live):
    w = [x * live for x in cubic_weights(fraction)]
    d = cell_of(iota((E, STEP), 0)) - (cells - 1)
    return jnp.where(
        d == 0, w[0], jnp.where(d == 1, w[1], jnp.where(d == 2, w[2], jnp.where(d == 3, w[3], 0.0)))
    )


def weights_kernel(points, after, r_high, r_low, r_twice, r_all, c_high, c_low, c_twice):
    kinds = Rows()
    for i in range(points.shape[1] // STEP):
        at = pl.ds(i * STEP, STEP)
        rows, cols, row_fracs, col_fracs, live, _ = fields(points, at)
        r_all[:, at] = stencil(rows, row_fracs, live)
        r_at, r_weights = touched(rows), weight_parts(row_fracs, live)
        r_high[:, at], r_low[:, at] = place(kinds.main, r_at, r_weights)
        r_twice[:, at] = kinds.pair(r_at, r_weights)
        c_at, c_weights = touched(cols), weight_parts(col_fracs)
        c_high[:, at], c_low[:, at] = place(kinds.main, c_at, c_weights)
        c_twice[:, at] = kinds.pair(c_at, c_weights)


def middle_kernel(
    spot, row, group, tail, far, near, yh, yl, scale, scale_tail, points, r_high, r_low, r_twice,
    r_all, c_high, c_low, c_twice, turned, ends, image, main_out, edge_out, far_out, near_out, main, edge,
):
    grid = grid_parts(row, group, tail, far, near, yh, yl, scale, scale_tail)
    kinds = Rows()
    for i in range(points.shape[1] // STEP):
        at = pl.ds(i * STEP, STEP)
        value = pick(grid, (c_high[:, at], c_low[:, at]), c_twice[:, at], r_all[:, at])
        image[:, at] = value
    for i in range(points.shape[1] // STEP):
        at = pl.ds(i * STEP, STEP)
        _, cols, _, col_fracs, _, _ = fields(points, at)
        c_weights = weight_parts(col_fracs, image[:, at])
        r_main = r_high[:, at], r_low[:, at]
        add_spread(i, kinds, r_main, r_twice[:, at], touched(cols), c_weights, main, edge)
    scaled_slabs(
        spot[0] == 0, main[...], edge[...], turned, ends[...], main_out, edge_out, far_out, near_out
    )


def last_kernel(
    row, group, tail, far, near, yh, yl, scale, scale_tail, r_all, c_high, c_low, c_twice, points, image,
    image_two, sums,
):
    grid = grid_parts(row, group, tail, far, near, yh, yl, scale, scale_tail)
    for i in range(r_all.shape[1] // STEP):
        at = pl.ds(i * STEP, STEP)
        image_two[:, at] = pick(grid, (c_high[:, at], c_low[:, at]), c_twice[:, at], r_all[:, at])
    b, v, w = points[5:6], image[...], image_two[...]
    lane = iota((1, 128), 1)
    total = jnp.zeros((1, 128), f32)
    for i, product in enumerate((b * b, b * v, v * v, v * w, w * w)):
        total = jnp.where(lane == i, jnp.sum(product, axis=1, keepdims=True), total)
    sums[...] = jnp.broadcast_to(total, sums.shape)


def finish_kernel(ridge, parts, points, image, image_two, solution_out, residual_out, relative_out):
    total = jnp.sum(parts[...], axis=0, keepdims=True)
    bb, bv, vv, vw, ww = (total[:, i : i + 1] for i in range(5))
    rho = ridge[0]
    b_image = bv + rho * bb
    one = bb / b_image
    keep = 1.0 - one * rho
    mid = keep * keep * bb - 2.0 * keep * one * bv + one * one * vv
    curve = keep * keep * bv - 2.0 * keep * one * vv + one * one * vw
    ratio = mid / bb
    two = mid / (curve + rho * mid - ratio * mid / one)
    side = keep + ratio
    on_b = keep - two * rho * side
    on_v = -one - two * (side - rho * one)
    on_w = two * one
    b, v, w = points[5:6], image[...], image_two[...]
    solution_out[...] = (one + two * side) * b - (two * one) * v
    residual_out[...] = on_b * b + on_v * v + on_w * w
    end = (
        on_b * on_b * bb
        + 2.0 * on_b * on_v * bv
        + (on_v * on_v + 2.0 * on_b * on_w) * vv
        + 2.0 * on_v * on_w * vw
        + on_w * on_w * ww
    )
    relative_out[...] = jnp.broadcast_to(end / bb, relative_out.shape)


def call(kernel, outs, args, scalars=(), scratch=(), mib=20, flops=0):
    vmem = pl.BlockSpec(memory_space=pltpu.VMEM)
    smem = pl.BlockSpec(memory_space=pltpu.SMEM)
    shapes = tuple(jax.ShapeDtypeStruct(shape, dtype) for shape, dtype in outs)
    return pl.pallas_call(
        kernel,
        out_shape=shapes,
        in_specs=[smem if i in scalars else vmem for i in range(len(args))],
        out_specs=tuple(vmem for _ in outs),
        scratch_shapes=list(scratch),
        compiler_params=pltpu.CompilerParams(vmem_limit_bytes=mib << 20),
        cost_estimate=pl.CostEstimate(flops=flops, bytes_accessed=1 << 20, transcendentals=0),
    )(*args)


def solution(mesh):
    gx, gy = mesh.axis_names

    def pairs(axis):
        count = mesh.shape[axis]
        near = [(i, i ^ 1) for i in range(count)]
        far = [(i, (i + 1) % count if i % 2 else (i - 1) % count) for i in range(count)]
        return far, near

    def swap(axis, far, near):
        far_to, near_to = pairs(axis)
        near = lax.ppermute(near, axis, near_to)
        far = lax.ppermute(far, axis, far_to)
        return far, near

    def shards(row_cells, col_cells, fracs, counts, targets, amplitude, lengthscale, ridge):
        n = targets.shape[2]
        spot = jnp.stack([lax.axis_index(gx) % 2, lax.axis_index(gy) % 2]).astype(jnp.int32)
        vector = ((1, n), f32)
        block = ((T, T), f32)
        main, edge = ((E, T), f32), ((8, 384), f32)
        slab, first_slab = ((SLAB, T), f32), ((SLAB + 16, T), f32)
        strip, corner = ((8, T), f32), ((8, 128), f32)
        row = ((T, 384), f32)
        scales = (main, ((E, 128), f32))
        scratch = (pltpu.VMEM((E, T), f32), pltpu.VMEM((8, 384), f32))

        ends = jnp.concatenate([amplitude[:8], amplitude[T - 8 :]], 0)
        alive = jnp.arange(n) < counts[0, 0]
        sources = [row_cells[0, 0].astype(f32), col_cells[0, 0].astype(f32)]
        sources += [fracs[0, 0, 0], fracs[1, 0, 0], jnp.ones((n,), f32), targets[0, 0]]
        known = [jnp.where(alive, x, 0.0) for x in sources]
        points = jnp.stack(known + [jnp.zeros((n,), f32)] * 2)
        far_end, near_end = swap(gy, ends, ends)
        bands = call(bands_kernel, (((E, K), bf16),) * 4, (spot, lengthscale), (0, 1))
        x_bands, y_bands = bands[:2], bands[2:]
        half, twice = ((T, n), bf16), ((16, n), bf16)
        inner, rim = call(
            spread_kernel,
            (main, edge),
            (points,),
            flops=6 << 28,
        )
        inner, rim, turned, ends, far, near = call(
            first_slabs_kernel,
            (main, edge, block, strip, first_slab, first_slab),
            (spot, inner, rim, amplitude, far_end, near_end),
            (0,),
        )
        far, near = swap(gx, far, near)
        *across, far, near, outside, ends_corner, scale, scale_tail = call(
            first_across_kernel,
            (row, edge, strip, slab, slab, strip, corner, *scales),
            (spot, inner, rim, amplitude, turned, ends, far, near, *x_bands),
            (0,),
        )
        matrices = call(
            weights_kernel,
            (half, half, twice, ((E, n), f32), half, half, twice),
            (points, ends_corner),
            flops=3 << 28,
        )
        far, near = swap(gy, far, near)
        image, inner, rim, far, near = call(
            middle_kernel,
            (vector, main, edge, slab, slab),
            (
                spot, *across, far, near, *y_bands, scale, scale_tail, points,
                *matrices, turned, ends,
            ),
            (0,),
            scratch,
        )
        far, near = swap(gx, far, near)
        *across, far, near = call(
            across_kernel,
            (row, edge, strip, slab, slab),
            (spot, inner, rim, turned, ends, outside, ends_corner, far, near, *x_bands),
            (0,),
        )
        far, near = swap(gy, far, near)
        devices = mesh.size
        image_two, sums = call(
            last_kernel,
            (vector, ((devices, 128), f32)),
            (*across, far, near, *y_bands, scale, scale_tail, *matrices[3:], points, image),
            (),
        )
        parts = lax.all_to_all(sums.reshape(devices, 1, 128), (gx, gy), 0, 0)
        out, residual, relative = call(
            finish_kernel,
            (vector, vector, ((1, 128), f32)),
            (ridge, parts.reshape(devices, 128), points, image, image_two),
            (0,),
        )
        return out.reshape(1, 1, n), residual.reshape(1, 1, n), relative[0, :1]

    tiles = P(gy, gx, None)
    return jax.shard_map(
        shards,
        mesh=mesh,
        in_specs=(tiles, tiles, P(None, gy, gx, None), P(gy, gx), tiles, P(gy, gx), P(), P()),
        out_specs=(tiles, tiles, P()),
        check_vma=False,
    )
```
